128 devices in a mesh: week: 4 (over x), row: 4 (over z), col: 8 (over y, core).
Axes of the slice: x: 4, y: 4, z: 4, core: 2. Of those that a mesh axis runs over, the one named last changes fastest.
Arguments:
- sensitivity: bfloat16 [4, 3, 1024, 4096], P('week', None, None, ('row', 'col')), may hold values from -0.1875 to 0.1875
- reach: int32 [4, 1024], P('week'), may hold values from 0 to 2, as said below
- obs_weight: float32 [4, 1024], P('week'), may hold values from 0.25 to 4
- prior_precision: float32 [4, 4096], P('week', ('row', 'col')), may hold values from 0.5 to 4
- pivot_solve: bfloat16 [4096, 4096], P('week', ('row', 'col')), may hold values from -0.09375 to 0.09375
Outputs:
- hessian_band: float32 [4, 3, 4096, 4096], P('week', None, ('row', 'col'))
- panel: bfloat16 [4096, 4096], P(('row', 'col'), 'week')
- schur: float32 [4096, 4096], P(('row', 'col'), 'week')
The draws below stay inside these ranges and needn't reach their ends.
Inputs may be any that keep to these rules, and one draw needn't show every extreme that they name: The number of observations at each reach differs widely from week to week; in some week w >= 2 every observation has reach 2.
All inputs are finite; a program needn't handle non-finite values.
Results may differ from the reference program's by a relative error of at most 0.013.
Values may be sent and summed in bfloat16 or wider, within the bound.
No kernel may reach another device: no remote copies, remote signals or barrier semaphores. Data moves between devices by JAX's collectives and lax.ppermute only.
A program may use at most 128 MiB of HBM per device.

```python
import math
import jax
import jax.numpy as jnp

REG = 4096
OBS = 1024
LAGS = 3
NW = 4
N_WEEK = 4


def draw_reach(key, part):
    base = jax.random.fold_in(key, 7)
    keys = jax.random.split(base, 7)
    heavy = LAGS - 1 + jax.random.randint(keys[0], (), 0, NW - LAGS + 1)
    light = jnp.where(heavy + 1 < NW, heavy + 1, heavy - 1)
    lower = jax.random.randint(keys[1], (NW, 1), 0, 1001)
    spread = jax.random.randint(keys[2], (NW, 1), 0, 1001)
    upper = jnp.minimum(lower + spread, 1000)
    unit = jax.random.randint(keys[3], (NW, OBS), 0, 1000)
    mixed = jnp.minimum((unit >= lower).astype(jnp.int32) + (unit >= upper).astype(jnp.int32), LAGS - 1)
    count = jax.random.randint(keys[4], (), 1, OBS // 8 + 1)
    order = jax.random.permutation(keys[5], OBS)
    low_reach = jax.random.randint(keys[6], (OBS,), 0, LAGS - 1)
    light_row = jnp.where(order < count, LAGS - 1, low_reach)
    weeks = jnp.arange(NW)[:, None]
    result = jnp.where(weeks == heavy, LAGS - 1, jnp.where(weeks == light, light_row[None, :], mixed))
    return result.astype(jnp.int32)


def block_scale(rng, dims, pieces, least, largest):
    factor_of = 1.0
    for axis_at, shards_of in pieces:
        steps = jax.random.uniform(jax.random.fold_in(jax.random.fold_in(rng, 6), axis_at), (shards_of,), jnp.float32, least / len(pieces), largest / len(pieces))
        factor_of = factor_of * jnp.repeat(jnp.exp(steps), dims[axis_at] // shards_of).reshape((-1,) + (1,) * (len(dims) - 1 - axis_at))
    return factor_of


def centred(key, shape, deviation, limit, shards=(), kind=jnp.bfloat16):
    level = block_scale(key, shape, shards, -0.22, 0.18) if shards else 1.0
    array = jax.random.normal(key, shape, jnp.float32) * deviation * level
    return jnp.minimum(jnp.maximum(array, -limit), limit).astype(kind)


def setup_inputs(seed: int = 0) -> dict:
    streams_of = jax.random.split(jax.random.key(seed), 6)
    return {
        "sensitivity": centred(streams_of[0], (NW, LAGS, OBS, REG), OBS ** -0.5, 0.1875, ((0, 4), (3, 32))),
        "reach": draw_reach(jax.random.fold_in(streams_of[5], 71), 0),
        "obs_weight": jnp.clip(jnp.exp(math.log(4.0) - 2.7725887 * jax.random.uniform(streams_of[2], (NW, OBS), jnp.float32) ** block_scale(streams_of[2], (NW, OBS), ((0, 4),), -0.2, 0.2)), 0.25, 4.0),
        "prior_precision": jnp.clip(jnp.exp(math.log(4.0) - 2.0794415 * jax.random.uniform(streams_of[3], (NW, REG), jnp.float32) ** block_scale(streams_of[3], (NW, REG), ((0, 4), (1, 32)), -0.2, 0.2)), 0.5, 4.0),
        "pivot_solve": centred(streams_of[4], (REG, REG), REG ** -0.5, 0.09375, ((0, 4), (1, 32))),
    }


def reference(sensitivity, reach, obs_weight, prior_precision, pivot_solve):
    block_rows = []
    for i in range(N_WEEK):
        blocks = []
        for d in range(LAGS):
            total = jnp.zeros((REG, REG), jnp.float32)
            if i - d >= 0:
                for a in range(LAGS - d):
                    w = i + a
                    b = a + d
                    if w < N_WEEK:
                        keep = (reach[w] >= b).astype(jnp.float32) * obs_weight[w]
                        scaled = (keep[:, None] * sensitivity[w, a].astype(jnp.float32)).astype(jnp.bfloat16)
                        total = total + jnp.dot(scaled.T, sensitivity[w, b], preferred_element_type=jnp.float32)
                if d == 0:
                    total = total + jnp.diag(prior_precision[i])
            blocks.append(total)
        block_rows.append(jnp.stack(blocks))
    hessian_band = jnp.stack(block_rows)
    coupling = hessian_band[1, 1].astype(jnp.bfloat16)
    panel = jnp.dot(coupling, pivot_solve.T, preferred_element_type=jnp.float32).astype(jnp.bfloat16)
    schur = hessian_band[1, 0] - jnp.dot(panel, panel.T, preferred_element_type=jnp.float32)
    return hessian_band, panel, schur
```

```python
import jax
import jax.numpy as jnp
from jax import lax
from jax.experimental import pallas as pl
from jax.experimental.pallas import tpu as pltpu
from jax.sharding import PartitionSpec as P

AXES = ("week", "row", "col")


def moved(block, sizes, dw=0, dz=0, dy=0, dk=0, weeks=None):
    n_week, n_row, n_col = sizes
    n_y = n_col // 2
    route = []
    for w in range(n_week):
        if weeks is not None and w not in weeks:
            continue
        for z in range(n_row):
            for y in range(n_y):
                for k in range(2):
                    here = (w * n_row + z) * n_col + y * 2 + k
                    to = (((w + dw) % n_week) * n_row + (z + dz) % n_row) * n_col
                    to += ((y + dy) % n_y) * 2 + (k + dk) % 2
                    route.append((here, to))
    return lax.ppermute(block, AXES, route)


def contract_first(left, right):
    return lax.dot_general(
        left, right, (((0,), (0,)), ((), ())), preferred_element_type=jnp.float32
    )


def contract_last(left, right):
    return lax.dot_general(
        left, right, (((1,), (1,)), ((), ())), preferred_element_type=jnp.float32
    )


def place_band(pieces, prior, zs, ys, n_row):
    lags, cores, slim, wide = pieces[0].shape
    n_y = len(pieces)
    width = n_y * cores * slim

    def kernel(zs_ref, ys_ref, *refs):
        ins, prior_ref, out_ref = refs[:n_y], refs[n_y], refs[n_y + 1]
        for t in range(n_y):
            for e in range(cores):
                at = pl.multiple_of(ys_ref[t * cores + e] * slim, slim)
                out_ref[0, :, pl.ds(at, slim)] = ins[t][0, e].astype(jnp.float32)

        @pl.when((pl.program_id(0) == 0) & (pl.program_id(1) == 0))
        def _():
            at = pl.multiple_of(ys_ref[0] * slim, slim)
            rows = lax.broadcasted_iota(jnp.int32, (slim, slim), 0)
            cols = lax.broadcasted_iota(jnp.int32, (slim, slim), 1)
            out_ref[0, :, pl.ds(at, slim)] += jnp.where(rows == cols, prior_ref[...], 0.0)

    grid_spec = pltpu.PrefetchScalarGridSpec(
        num_scalar_prefetch=2,
        grid=(lags, n_row),
        in_specs=[
            pl.BlockSpec((1, cores, slim, slim), lambda d, s, zr, yr: (d, 0, 0, s))
            for _ in range(n_y)
        ]
        + [pl.BlockSpec((1, slim), lambda d, s, zr, yr: (0, 0))],
        out_specs=pl.BlockSpec((1, slim, width), lambda d, s, zr, yr: (d, 0, zr[s])),
    )
    return pl.pallas_call(
        kernel,
        grid_spec=grid_spec,
        out_shape=jax.ShapeDtypeStruct((lags, slim, n_row * width), jnp.float32),
        name="place_band",
    )(zs, ys, *pieces, prior)


def body(sensitivity, reach, obs_weight, prior_precision, pivot_solve):
    sizes = tuple(lax.axis_size(a) for a in AXES)
    n_week, n_row, n_col = sizes
    n_y = n_col // 2
    week = lax.axis_index("week")
    z = lax.axis_index("row")
    col = lax.axis_index("col")
    y, k = col // 2, col % 2
    local = sensitivity[0]
    lags, obs, slim = local.shape
    bf = jnp.bfloat16
    f32 = jnp.float32

    def move(block, **by):
        return moved(block, sizes, **by)

    def over_z(block, weeks=None):
        return [block] + [move(block, dz=s, weeks=weeks) for s in range(1, n_row)]

    def over_y(block, weeks=None):
        own = [block] + [move(block, dy=t, weeks=weeks) for t in range(1, n_y)]
        mine = jnp.stack(own)
        other = move(mine, dk=1, weeks=weeks)
        return own + [other[t] for t in range(n_y)]

    def lanes(blocks):
        return jnp.concatenate(blocks, axis=-1)

    root = jnp.sqrt(obs_weight[0])
    lag_ids = lax.broadcasted_iota(jnp.int32, (lags, obs), 0)
    keep = jnp.where((reach[0][None] >= lag_ids) & (week >= lag_ids), root[None], 0.0)
    held = (keep[:, :, None] * local.astype(f32)).astype(bf)

    pair = lax.dynamic_slice_in_dim(held, jnp.where(week == 1, 0, 1), 2, 0)
    below = move(pair, dw=-1, weeks=(1, 2, 3))
    above = move(pair, dw=1, weeks=(1, 2))
    across = move(pair, dw=2, weeks=(1, 2))
    far = move(held[2], dw=-2, weeks=(3,))
    pivot = lanes(over_z(pivot_solve))
    own_right = over_z(held[0])

    def by_week(*choices):
        return lax.select_n(week, *choices)

    first = by_week(below, pair, pair, above)
    second = by_week(across, below, above, across)

    left_c = over_y(jnp.concatenate([first[0], second[0]]))
    right_c = over_z(jnp.concatenate([first[1], second[1]]))
    left_c = lanes(left_c)
    right_c = lanes(right_c)
    coupling_here = contract_first(left_c, right_c)
    coupling = coupling_here.astype(bf)

    half = n_y * slim
    part = contract_last(coupling, pivot)
    summed = part[:half] + move(part[half:].astype(bf), dk=1).astype(f32)
    panel_sum = summed[:slim]
    for t in range(1, n_y):
        sent = summed[t * slim : (t + 1) * slim].astype(bf)
        panel_sum = panel_sum + move(sent, dy=-t).astype(f32)
    panel = panel_sum.astype(bf)

    left_0 = over_y(held[0], weeks=(0, 2, 3))
    left_1 = over_y(by_week(below[1], far, below[0], far), weeks=(0, 1, 2))
    left_2 = over_y(across[1], weeks=(0,))
    right_12 = over_z(held[1:3].reshape(2 * obs, slim), weeks=(2, 3))
    foreign = by_week(below, jnp.stack([below[0], far]), below, below)
    right_f = over_z(foreign.reshape(2 * obs, slim), weeks=(1, 2))
    left_0, left_1, left_2 = lanes(left_0), lanes(left_1), lanes(left_2)
    right_0, right_12, right_f = lanes(own_right), lanes(right_12), lanes(right_f)
    rows = n_col * slim
    cols = n_row * slim

    def week_0(lc, rc, cc, l0, l1, l2, r0, r12, rf):
        h0 = contract_first(l0, r0) + contract_first(l1, rc[:obs]) + contract_first(l2, rc[obs:])
        none = jnp.zeros((rows, cols), bf)
        return jnp.stack([h0.astype(bf), none, none])

    def week_1(lc, rc, cc, l0, l1, l2, r0, r12, rf):
        h0 = contract_first(lc[:obs], r0) + contract_first(lc[obs:], rf[:obs])
        h0 = h0 + contract_first(l1, rf[obs:])
        return jnp.stack([h0.astype(bf), cc, jnp.zeros((rows, cols), bf)])

    def week_2(lc, rc, cc, l0, l1, l2, r0, r12, rf):
        h0 = contract_first(l0, r0) + contract_first(l1, rf[:obs])
        h1 = contract_first(l0, r12[:obs]) + contract_first(l1, rf[obs:])
        h2 = contract_first(l0, rc[:obs])
        return jnp.stack([h0.astype(bf), h1.astype(bf), h2.astype(bf)])

    def week_3(lc, rc, cc, l0, l1, l2, r0, r12, rf):
        h0 = contract_first(l0, r0)
        h1 = contract_first(l0, r12[:obs])
        h2 = contract_first(l0, r12[obs:])
        return jnp.stack([h0.astype(bf), h1.astype(bf), h2.astype(bf)])

    blocks = lax.switch(
        week, (week_0, week_1, week_2, week_3),
        left_c, right_c, coupling, left_0, left_1, left_2, right_0, right_12, right_f,
    )

    left_p = jnp.concatenate(over_y(panel), axis=0)
    slots = jnp.stack(over_z(panel))
    ordered = [
        lax.dynamic_index_in_dim(slots, (z - week - j) % n_row, 0, keepdims=False)
        for j in range(n_week)
    ]
    gram = contract_last(left_p, jnp.concatenate(ordered, axis=0))
    here = blocks[0].astype(f32)
    eye = lax.broadcasted_iota(jnp.int32, (slim, slim), 0) == lax.broadcasted_iota(
        jnp.int32, (slim, slim), 1
    )
    corner = jnp.where(eye, prior_precision[0][None, :], 0.0)
    here = here.at[:slim, :slim].add(corner)
    here = here.reshape(rows, n_row, slim)
    here = lanes(
        [
            lax.dynamic_index_in_dim(here, (z - week - j) % n_row, 1, keepdims=False)
            for j in range(n_week)
        ]
    )
    term = jnp.where(week == 1, here, 0.0) - gram
    total = term[:, :slim]
    for j in range(1, n_week):
        sent = term[:, j * slim : (j + 1) * slim].astype(bf)
        total = total + move(sent, dw=j).astype(f32)
    total = total.astype(bf)
    other = move(total[half:], dk=1)
    both = jnp.stack([total[:half], other]).reshape(2, n_y, slim, slim)
    arrived = [both[:, 0]]
    for t in range(1, n_y):
        arrived.append(move(both[:, t], dy=-t))

    places = [((y + t) % n_y) * 2 + (k + e) % 2 for t in range(n_y) for e in range(2)]
    ys = jnp.stack(places).astype(jnp.int32)
    schur = jnp.zeros((slim, n_col * slim), f32)
    for t in range(n_y):
        for e in range(2):
            schur = lax.dynamic_update_slice_in_dim(
                schur, arrived[t][e].astype(f32), places[t * 2 + e] * slim, 1
            )

    blocks = blocks.reshape(lags, 2, half, cols)
    other = move(blocks[:, 1], dk=1)
    both = jnp.stack([blocks[:, 0], other], axis=1).reshape(lags, 2, n_y, slim, cols)
    pieces = [both[:, :, 0]]
    for t in range(1, n_y):
        pieces.append(move(both[:, :, t], dy=-t))
    zs = jnp.stack([(z - s) % n_row for s in range(n_row)]).astype(jnp.int32)
    bands = place_band(pieces, prior_precision, zs, ys, n_row)
    return (bands[None], panel, schur)


def solution(mesh):
    placed = (
        P("week", None, None, ("row", "col")),
        P("week", None),
        P("week", None),
        P("week", ("row", "col")),
        P("week", ("row", "col")),
    )
    return jax.shard_map(
        body,
        mesh=mesh,
        in_specs=placed,
        out_specs=(
            P("week", None, ("row", "col"), None),
            P(("row", "col"), "week"),
            P(("row", "col"), "week"),
        ),
        check_vma=False,
    )
```

```python
import jax
import jax.numpy as jnp
from jax import lax
from jax.experimental import pallas as pl
from jax.experimental.pallas import tpu as pltpu
from jax.sharding import PartitionSpec as P

AXES = ("week", "row", "col")


def moved(block, sizes, dw=0, dz=0, dy=0, dk=0, weeks=None):
    n_week, n_row, n_col = sizes
    n_y = n_col // 2
    route = []
    for w in range(n_week):
        if weeks is not None and w not in weeks:
            continue
        for z in range(n_row):
            for y in range(n_y):
                for k in range(2):
                    here = (w * n_row + z) * n_col + y * 2 + k
                    to = (((w + dw) % n_week) * n_row + (z + dz) % n_row) * n_col
                    to += ((y + dy) % n_y) * 2 + (k + dk) % 2
                    route.append((here, to))
    return lax.ppermute(block, AXES, route)


HBM = pl.BlockSpec(memory_space=pl.ANY)
VMEM = pl.BlockSpec(memory_space=pltpu.VMEM)
SMEM = pl.BlockSpec(memory_space=pltpu.SMEM)
LIMIT = pltpu.CompilerParams(vmem_limit_bytes=48 * 1024 * 1024)
bf = jnp.bfloat16
f32 = jnp.float32


def contract_first(left, right):
    return lax.dot_general(
        left, right, (((0,), (0,)), ((), ())), preferred_element_type=jnp.float32
    )


def dot_first(left, right):
    return lax.dot_general(
        left, right, (((0,), (0,)), ((), ())), preferred_element_type=jnp.float32
    )


def dot_last(left, right):
    return lax.dot_general(
        left, right, (((1,), (1,)), ((), ())), preferred_element_type=jnp.float32
    )


def brought(copies, sems):
    started = []
    for n, (source, target) in enumerate(copies):
        copy = pltpu.make_async_copy(source, target, sems.at[n])
        copy.start()
        started.append(copy)
    for copy in started:
        copy.wait()


def left_copies(pieces, scratch, a, obs, slim):
    rows = pl.ds(a * obs, obs)
    return [
        (ref, scratch.at[t // 2, rows, pl.ds((t % 2) * slim, slim)])
        for t, ref in enumerate(pieces)
    ]


def right_copies(pieces, scratch, a, obs, slim):
    rows = pl.ds(a * obs, obs)
    return [(ref, scratch.at[rows, pl.ds(n * slim, slim)]) for n, ref in enumerate(pieces)]


def cut(refs, *lengths):
    parts, at = [], 0
    for length in lengths:
        parts.append(refs[at : at + length])
        at += length
    return parts + [refs[at:]]


def coupling_and_parts(lefts, rights, pivots):
    n_a, obs, slim = rights[0].shape
    n_r, n_c, wide = len(lefts), len(rights), pivots[0].shape[0]
    pairs = n_r // 2

    def kernel(*refs):
        la, ra, pv, rest = cut(refs, n_r, n_c, n_c)
        parts, (l_s, r_s, p_s, sems) = rest[:n_r], rest[n_r:]
        copies = right_copies(pv, p_s, 0, wide, slim)
        for a in range(n_a):
            copies += left_copies([ref.at[a] for ref in la], l_s, a, obs, slim)
            copies += right_copies([ref.at[a] for ref in ra], r_s, a, obs, slim)
        brought(copies, sems)
        for n in range(pairs):
            block = dot_first(l_s[n], r_s[...]).astype(bf)
            part = dot_last(block, p_s[...])
            for m in range(2):
                out = parts[2 * n + m]
                out[...] = part[m * slim : (m + 1) * slim].astype(out.dtype)

    operands = [*lefts, *rights, *pivots]
    return pl.pallas_call(
        kernel,
        in_specs=[VMEM] * len(operands),
        out_specs=[VMEM] * n_r,
        out_shape=[jax.ShapeDtypeStruct((slim, wide), bf if t else f32) for t in range(n_r)],
        scratch_shapes=[
            pltpu.VMEM((pairs, n_a * obs, 2 * slim), bf),
            pltpu.VMEM((n_a * obs, n_c * slim), bf),
            pltpu.VMEM((wide, n_c * slim), bf),
            pltpu.SemaphoreType.DMA((n_a * (n_r + n_c) + n_c,)),
        ],
        compiler_params=LIMIT,
        name="coupling_and_parts",
    )(*operands)


def gram_terms(turn, rows_of, slots):
    slim, wide = slots[0].shape
    n_r, n_c = len(rows_of), len(slots)
    pairs, n_j = n_r // 2, n_c // 2

    def kernel(*refs):
        (turn_ref,), l_refs, r_refs, rest = cut(refs, 1, n_r, n_c)
        outs, (l_s, r_s, g_s, sems) = rest[:n_j], rest[n_j:]
        brought(
            [(ref, l_s.at[pl.ds(n * slim, slim)]) for n, ref in enumerate(l_refs)]
            + [(ref, r_s.at[pl.ds(n * slim, slim)]) for n, ref in enumerate(r_refs)],
            sems,
        )
        for n in range(pairs):
            gram = dot_last(l_s[pl.ds(n * 2 * slim, 2 * slim)], r_s[...])
            for e in range(2):
                for s in range(n_j):
                    at = (e * n_j + s) * slim
                    rows, lanes = pl.ds(n * 2 * slim, 2 * slim), pl.ds(e * slim, slim)
                    g_s[s, rows, lanes] = gram[:, at : at + slim]
        for j in range(n_j):
            outs[j][...] = g_s[(turn_ref[0] + n_j - j) % n_j].astype(outs[j].dtype)

    operands = [*rows_of, *slots]
    return pl.pallas_call(
        kernel,
        in_specs=[SMEM] + [VMEM] * len(operands),
        out_specs=[VMEM] * n_j,
        out_shape=[
            jax.ShapeDtypeStruct((n_r * slim, 2 * slim), bf if j else f32) for j in range(n_j)
        ],
        scratch_shapes=[
            pltpu.VMEM((n_r * slim, wide), bf),
            pltpu.VMEM((n_c * slim, wide), bf),
            pltpu.VMEM((n_j, n_r * slim, 2 * slim), f32),
            pltpu.SemaphoreType.DMA((len(operands),)),
        ],
        compiler_params=LIMIT,
        name="gram_terms",
    )(turn.reshape(1), *operands)


def week_sum(terms, n_r):
    rows, wide = terms[0].shape
    slim = rows // n_r

    def kernel(*refs):
        ins, outs = refs[: len(terms)], refs[len(terms) :]
        for n in range(n_r):
            at = pl.ds(n * slim, slim)
            total = ins[0][at].astype(f32)
            for ref in ins[1:]:
                total = total + ref[at].astype(f32)
            outs[n][...] = total.astype(bf)

    return pl.pallas_call(
        kernel,
        in_specs=[VMEM] * len(terms),
        out_specs=[VMEM] * n_r,
        out_shape=[jax.ShapeDtypeStruct((slim, wide), bf)] * n_r,
        name="week_sum",
    )(*terms)


def place_schur(ys, here, pieces):
    slim = pieces[0].shape[0]
    n = len(pieces)

    def kernel(ys_ref, here_ref, *refs):
        for t in range(n):
            for e in range(2):
                at = pl.ds(pl.multiple_of(ys_ref[2 * t + e] * slim, slim), slim)
                block = refs[t][:, e * slim : (e + 1) * slim]
                refs[-1][:, at] = here_ref[:, at] - block.astype(f32)

    return pl.pallas_call(
        kernel,
        in_specs=[SMEM] + [VMEM] * (1 + n),
        out_specs=VMEM,
        out_shape=jax.ShapeDtypeStruct((slim, 2 * n * slim), f32),
        name="place_schur",
    )(ys, here, *pieces)


def body(sensitivity, reach, obs_weight, prior_precision, pivot_solve):
    sizes = tuple(lax.axis_size(a) for a in AXES)
    n_week, n_row, n_col = sizes
    n_y = n_col // 2
    week = lax.axis_index("week")
    z = lax.axis_index("row")
    col = lax.axis_index("col")
    y, k = col // 2, col % 2
    local = sensitivity[0]
    lags, obs, slim = local.shape

    def move(block, **by):
        return moved(block, sizes, **by)

    def over_y(block):
        return [block] + [move(block, dy=t) for t in range(1, n_y)]

    def over_z(block):
        own = [block] + [move(block, dz=s) for s in range(1, n_row)]
        return own + [move(p, dk=1) for p in own]

    def to_rows(blocks):
        return [blocks[0]] + [move(blocks[t], dy=-t) for t in range(1, n_y)]

    def after(value, *events):
        return lax.optimization_barrier((value, *events))[0]

    def by_week(*choices):
        return lax.select_n(week, *choices)

    pivots = over_z(pivot_solve)

    root = jnp.sqrt(obs_weight[0])

    def scaled(lag):
        keep = jnp.where((reach[0] >= lag) & (week >= lag), root, 0.0)
        return (keep[:, None] * local[lag].astype(f32)).astype(bf)

    held = [scaled(lag) for lag in range(lags)]
    pair = jnp.stack(
        [by_week(held[1], held[0], held[1], held[1]), by_week(held[2], held[1], held[2], held[2])]
    )
    below = move(pair, dw=-1, weeks=(1, 2, 3))
    above = move(pair, dw=1, weeks=(1, 2))
    across = move(pair, dw=2, weeks=(1, 2))
    wide = [lax.all_gather(held[lag], ("row", "col"), axis=1, tiled=True) for lag in (2, 1, 0)]

    def both(n):
        first = by_week(below[n], pair[n], pair[n], above[n])
        return jnp.stack([first, by_week(across[n], below[n], above[n], across[n])])

    left_c, right_c = over_y(both(0)), over_z(both(1))
    parts = coupling_and_parts(left_c, right_c, pivots)

    panel = parts[0]
    for t in range(1, n_y):
        panel = panel + move(parts[t], dy=-t).astype(f32)
    panel = panel.astype(bf)
    rows_of = over_y(panel)
    slots = over_z(panel)

    terms = gram_terms((z - week + n_week) % n_week, rows_of, slots)
    terms = [terms[0]] + [move(terms[j], dw=j) for j in range(1, n_week)]
    totals = to_rows(week_sum(terms, n_y))

    mine = after(jnp.concatenate(held[::-1], axis=1), parts[0])
    from_2 = contract_first(mine, wide[0])
    near = move(from_2[slim : 2 * slim].astype(bf), dw=-1, weeks=(2, 3)).astype(f32)
    far = move(from_2[:slim].astype(bf), dw=-2, weeks=(2, 3)).astype(f32)
    from_1 = contract_first(after(mine[:, slim:], panel, near), wide[1])
    next_0 = move(from_1[:slim].astype(bf), dw=-1, weeks=(1, 2, 3)).astype(f32)
    band_2 = from_2[2 * slim :]
    band_1 = from_1[slim:] + near
    from_0 = contract_first(after(held[0], terms[0]), wide[2])
    first = (lax.axis_index("row") * n_col + col) * slim
    rows = lax.broadcasted_iota(jnp.int32, (slim, n_row * n_col * slim), 0)
    cols = lax.broadcasted_iota(jnp.int32, (slim, n_row * n_col * slim), 1)
    diagonal = jnp.where(cols == rows + first, prior_precision[0][:, None], 0.0)
    band_0 = from_0 + next_0 + far + diagonal
    bands = jnp.stack([band_0, band_1, band_2])

    span = n_col * slim
    here = jnp.where(week == 1, band_0[:, span : 2 * span], 0.0)
    for j in range(1, n_week):
        at = (1 + j) % n_week * span
        here = here + move(band_0[:, at : at + span].astype(bf), dw=j, weeks=(1,)).astype(f32)

    ys = [((y + t) % n_y) * 2 + (k + e) % 2 for t in range(n_y) for e in range(2)]
    schur = place_schur(jnp.stack(ys).astype(jnp.int32), here, totals)
    return (bands[None], panel, schur)


def solution(mesh):
    placed = (
        P("week", None, None, ("row", "col")),
        P("week", None),
        P("week", None),
        P("week", ("row", "col")),
        P("week", ("row", "col")),
    )
    return jax.shard_map(
        body,
        mesh=mesh,
        in_specs=placed,
        out_specs=(
            P("week", None, ("row", "col"), None),
            P(("row", "col"), "week"),
            P(("row", "col"), "week"),
        ),
        check_vma=False,
    )
```

```python
import jax
import jax.numpy as jnp
from jax import lax
from jax.experimental import pallas as pl
from jax.experimental.pallas import tpu as pltpu
from jax.sharding import PartitionSpec as P

AXES = ("week", "row", "col")


def moved(block, sizes, dw=0, dz=0, dy=0, dk=0, weeks=None):
    n_week, n_row, n_col = sizes
    n_y = n_col // 2
    route = []
    for w in range(n_week):
        if weeks is not None and w not in weeks:
            continue
        for z in range(n_row):
            for y in range(n_y):
                for k in range(2):
                    here = (w * n_row + z) * n_col + y * 2 + k
                    to = (((w + dw) % n_week) * n_row + (z + dz) % n_row) * n_col
                    to += ((y + dy) % n_y) * 2 + (k + dk) % 2
                    route.append((here, to))
    return lax.ppermute(block, AXES, route)


HBM = pl.BlockSpec(memory_space=pl.ANY)
VMEM = pl.BlockSpec(memory_space=pltpu.VMEM)
SMEM = pl.BlockSpec(memory_space=pltpu.SMEM)
LIMIT = pltpu.CompilerParams(vmem_limit_bytes=48 * 1024 * 1024)
bf = jnp.bfloat16
f32 = jnp.float32


def dot_first(left, right):
    return lax.dot_general(
        left, right, (((0,), (0,)), ((), ())), preferred_element_type=jnp.float32
    )


def dot_last(left, right):
    return lax.dot_general(
        left, right, (((1,), (1,)), ((), ())), preferred_element_type=jnp.float32
    )


def brought(copies, sems):
    started = []
    for n, (source, target) in enumerate(copies):
        copy = pltpu.make_async_copy(source, target, sems.at[n])
        copy.start()
        started.append(copy)
    for copy in started:
        copy.wait()


def left_copies(pieces, scratch, a, obs, slim):
    rows = pl.ds(a * obs, obs)
    return [
        (ref, scratch.at[t // 2, rows, pl.ds((t % 2) * slim, slim)])
        for t, ref in enumerate(pieces)
    ]


def right_copies(pieces, scratch, a, obs, slim):
    rows = pl.ds(a * obs, obs)
    return [(ref, scratch.at[rows, pl.ds(n * slim, slim)]) for n, ref in enumerate(pieces)]


def cut(refs, *lengths):
    parts, at = [], 0
    for length in lengths:
        parts.append(refs[at : at + length])
        at += length
    return parts + [refs[at:]]


def coupling_and_parts(lefts, rights, pivots):
    obs, slim = rights[0].shape[1:]
    n_r, n_c, wide = len(lefts), len(rights), pivots[0].shape[0]
    pairs = n_r // 2
    operands, places = list(pivots), []
    for piece in [*lefts, *rights]:
        places.append((len(operands), isinstance(piece, tuple)))
        operands += piece if isinstance(piece, tuple) else [piece]
    n_in = len(operands)

    def kernel(*refs):
        parts, (l_s, r_s, p_s, sems) = refs[n_in : n_in + n_r], refs[n_in + n_r :]
        copies = right_copies(refs[:n_c], p_s, 0, wide, slim)
        for a in range(2):
            blocks = [refs[at + a] if two else refs[at].at[a] for at, two in places]
            copies += left_copies(blocks[:n_r], l_s, a, obs, slim)
            copies += right_copies(blocks[n_r:], r_s, a, obs, slim)
        brought(copies, sems)
        for n in range(pairs):
            block = dot_first(l_s[n], r_s[...]).astype(bf)
            part = dot_last(block, p_s[...])
            for m in range(2):
                out = parts[2 * n + m]
                out[...] = part[m * slim : (m + 1) * slim].astype(out.dtype)

    return pl.pallas_call(
        kernel,
        in_specs=[VMEM] * n_in,
        out_specs=[VMEM] * n_r,
        out_shape=[jax.ShapeDtypeStruct((slim, wide), bf if t else f32) for t in range(n_r)],
        scratch_shapes=[
            pltpu.VMEM((pairs, 2 * obs, 2 * slim), bf),
            pltpu.VMEM((2 * obs, n_c * slim), bf),
            pltpu.VMEM((wide, n_c * slim), bf),
            pltpu.SemaphoreType.DMA((2 * (n_r + n_c) + n_c,)),
        ],
        compiler_params=LIMIT,
        name="coupling_and_parts",
    )(*operands)


def gram_terms(turn, rows_of, slots):
    slim, wide = slots[0].shape
    n_r, n_c = len(rows_of), len(slots)
    pairs, n_j = n_r // 2, n_c // 2

    def kernel(*refs):
        (turn_ref,), l_refs, r_refs, rest = cut(refs, 1, n_r, n_c)
        outs, (l_s, r_s, g_s, sems) = rest[:n_j], rest[n_j:]
        brought(
            [(ref, l_s.at[pl.ds(n * slim, slim)]) for n, ref in enumerate(l_refs)]
            + [(ref, r_s.at[pl.ds(n * slim, slim)]) for n, ref in enumerate(r_refs)],
            sems,
        )
        for n in range(pairs):
            gram = dot_last(l_s[pl.ds(n * 2 * slim, 2 * slim)], r_s[...])
            for e in range(2):
                for s in range(n_j):
                    at = (e * n_j + s) * slim
                    rows, lanes = pl.ds(n * 2 * slim, 2 * slim), pl.ds(e * slim, slim)
                    g_s[s, rows, lanes] = gram[:, at : at + slim]
        for j in range(n_j):
            outs[j][...] = g_s[(turn_ref[0] + n_j - j) % n_j].astype(outs[j].dtype)

    operands = [*rows_of, *slots]
    return pl.pallas_call(
        kernel,
        in_specs=[SMEM] + [VMEM] * len(operands),
        out_specs=[VMEM] * n_j,
        out_shape=[
            jax.ShapeDtypeStruct((n_r * slim, 2 * slim), bf if j else f32) for j in range(n_j)
        ],
        scratch_shapes=[
            pltpu.VMEM((n_r * slim, wide), bf),
            pltpu.VMEM((n_c * slim, wide), bf),
            pltpu.VMEM((n_j, n_r * slim, 2 * slim), f32),
            pltpu.SemaphoreType.DMA((len(operands),)),
        ],
        compiler_params=LIMIT,
        name="gram_terms",
    )(turn.reshape(1), *operands)


def week_sum(terms, n_r):
    rows, wide = terms[0].shape
    slim = rows // n_r

    def kernel(*refs):
        ins, outs = refs[: len(terms)], refs[len(terms) :]
        for n in range(n_r):
            at = pl.ds(n * slim, slim)
            total = ins[0][at].astype(f32)
            for ref in ins[1:]:
                total = total + ref[at].astype(f32)
            outs[n][...] = total.astype(bf)

    return pl.pallas_call(
        kernel,
        in_specs=[VMEM] * len(terms),
        out_specs=[VMEM] * n_r,
        out_shape=[jax.ShapeDtypeStruct((slim, wide), bf)] * n_r,
        name="week_sum",
    )(*terms)


def band_products(week, left, wide):
    n_b, obs, regions = wide.shape
    slim = left.shape[1] // 2
    tile = min(512, regions // 4)

    def kernel(week_ref, left_ref, wide_ref, band_ref, send_a, send_b, turned):
        @pl.when(pl.program_id(0) == 0)
        def _():
            turned[...] = left_ref[...].T

        from_a = jnp.dot(turned[...], wide_ref[0], preferred_element_type=f32)
        from_b = jnp.dot(turned[...], wide_ref[1], preferred_element_type=f32)
        late = week_ref[0] >= 2
        band_ref[0] = jnp.where(late, 0.0, from_a[:slim])
        band_ref[1] = from_b[:slim]
        band_ref[2] = jnp.where(late, from_a[:slim], 0.0)
        send_a[...] = from_a[slim:].astype(bf)
        send_b[...] = from_b[slim:].astype(bf)

    return pl.pallas_call(
        kernel,
        grid=(regions // tile,),
        in_specs=[SMEM, VMEM, pl.BlockSpec((n_b, obs, tile), lambda i: (0, 0, i))],
        out_specs=[
            pl.BlockSpec((3, slim, tile), lambda i: (0, 0, i)),
            pl.BlockSpec((slim, tile), lambda i: (0, i)),
            pl.BlockSpec((slim, tile), lambda i: (0, i)),
        ],
        out_shape=[
            jax.ShapeDtypeStruct((3, slim, regions), f32),
            jax.ShapeDtypeStruct((slim, regions), bf),
            jax.ShapeDtypeStruct((slim, regions), bf),
        ],
        scratch_shapes=[pltpu.VMEM((2 * slim, obs), bf)],
        compiler_params=LIMIT,
        name="band_products",
    )(week.reshape(1), left, wide)


def add_lag_1(bands, arrived):
    _, slim, regions = bands.shape
    tile = min(2048, regions)

    def kernel(band_ref, arrived_ref, out_ref):
        out_ref[0] = band_ref[0] + arrived_ref[...].astype(f32)

    band = pl.BlockSpec((1, slim, tile), lambda i: (1, 0, i))
    return pl.pallas_call(
        kernel,
        grid=(regions // tile,),
        in_specs=[band, pl.BlockSpec((slim, tile), lambda i: (0, i))],
        out_specs=band,
        out_shape=jax.ShapeDtypeStruct(bands.shape, f32),
        input_output_aliases={0: 0},
        name="add_lag_1",
    )(bands, arrived)


def finish_lag_0(first, left, wide, bands, arrived, prior, spans):
    obs, slim = left.shape
    regions = wide.shape[1]
    tile = min(512, regions // 4)
    span = regions // spans
    each = span // tile

    def kernel(first_ref, left_ref, wide_ref, band_ref, arrived_ref, prior_ref, out_ref, cut_ref, turned):
        step = pl.program_id(0)

        @pl.when(step == 0)
        def _():
            turned[...] = left_ref[...].T

        last = jnp.dot(turned[...], wide_ref[...], preferred_element_type=f32)
        rows = lax.broadcasted_iota(jnp.int32, (slim, tile), 0) + first_ref[0]
        cols = lax.broadcasted_iota(jnp.int32, (slim, tile), 1) + step * tile
        total = band_ref[0] + arrived_ref[...].astype(f32) + last
        total = total + jnp.where(rows == cols, prior_ref[...], 0.0)
        out_ref[0] = total
        cut_ref[0] = total.astype(bf)

    band = pl.BlockSpec((1, slim, tile), lambda i: (0, 0, i))
    return pl.pallas_call(
        kernel,
        grid=(regions // tile,),
        in_specs=[
            SMEM,
            VMEM,
            pl.BlockSpec((obs, tile), lambda i: (0, i)),
            band,
            pl.BlockSpec((slim, tile), lambda i: (0, i)),
            VMEM,
        ],
        out_specs=[band, pl.BlockSpec((1, slim, tile), lambda i: (i // each, 0, i % each))],
        out_shape=[
            jax.ShapeDtypeStruct(bands.shape, f32),
            jax.ShapeDtypeStruct((spans, slim, span), bf),
        ],
        scratch_shapes=[pltpu.VMEM((slim, obs), bf)],
        input_output_aliases={3: 0},
        compiler_params=LIMIT,
        name="finish_lag_0",
    )(first.reshape(1), left, wide, bands, arrived, prior.reshape(slim, 1))


def place_schur(ys, week, here, arrived, pieces):
    slim = pieces[0].shape[0]
    n, m = len(pieces), len(arrived)

    def kernel(ys_ref, week_ref, here_ref, *refs):
        own = week_ref[0] == 1
        for t in range(n):
            for e in range(2):
                at = pl.ds(pl.multiple_of(ys_ref[2 * t + e] * slim, slim), slim)
                total = -refs[m + t][:, e * slim : (e + 1) * slim].astype(f32)
                total = total + jnp.where(own, here_ref[1, :, at].astype(f32), 0.0)
                for ref in refs[:m]:
                    total = total + ref[:, at].astype(f32)
                refs[-1][:, at] = total

    return pl.pallas_call(
        kernel,
        in_specs=[SMEM, SMEM] + [VMEM] * (1 + m + n),
        out_specs=VMEM,
        out_shape=jax.ShapeDtypeStruct((slim, 2 * n * slim), f32),
        name="place_schur",
    )(ys, week.reshape(1), here, *arrived, *pieces)


def body(sensitivity, reach, obs_weight, prior_precision, pivot_solve):
    sizes = tuple(lax.axis_size(a) for a in AXES)
    n_week, n_row, n_col = sizes
    n_y = n_col // 2
    week = lax.axis_index("week")
    z = lax.axis_index("row")
    col = lax.axis_index("col")
    y, k = col // 2, col % 2
    local = sensitivity[0]
    lags, obs, slim = local.shape

    def move(block, **by):
        return moved(block, sizes, **by)

    def over_y(block):
        return [block] + [move(block, dy=t) for t in range(1, n_y)]

    def over_z(block):
        own = [block] + [move(block, dz=s) for s in range(1, n_row)]
        return own + [move(p, dk=1) for p in [after(block, own[1])] + own[1:]]

    def to_rows(blocks):
        return [blocks[0]] + [move(blocks[t], dy=-t) for t in range(1, n_y)]

    def after(value, *events):
        return lax.optimization_barrier((value, *events))[0]

    def by_week(*choices):
        return lax.select_n(week, *choices)

    pivots = over_z(pivot_solve)

    root = jnp.sqrt(obs_weight[0])

    def scaled(lag):
        keep = jnp.where((reach[0] >= lag) & (week >= lag), root, 0.0)
        return (keep[:, None] * local[lag].astype(f32)).astype(bf)

    held = [scaled(lag) for lag in range(lags)]
    pair = jnp.stack(
        [by_week(held[1], held[0], held[1], held[1]), by_week(held[2], held[1], held[2], held[2])]
    )
    below = move(pair, dw=-1, weeks=(1, 2, 3))
    above = move(pair, dw=1, weeks=(1, 2))
    across = move(pair, dw=2, weeks=(1, 2, 3))
    wide = jnp.stack([by_week(held[0], held[0], held[2], held[2]), held[1]])
    wide = lax.all_gather(wide, ("row", "col"), axis=2, tiled=True)
    def both(n):
        first = by_week(below[n], pair[n], pair[n], above[n])
        return jnp.stack([first, by_week(across[n], below[n], above[n], across[n])])

    left_c, right_c = over_y(both(0)), over_z(both(1))
    parts = coupling_and_parts(left_c, right_c, pivots)

    last = by_week(across[1], across[1], held[0], held[0])
    last = after(last, parts[0])
    wide_last = lax.all_gather(last, ("row", "col"), axis=1, tiled=True)

    panel = parts[0]
    for t in range(1, n_y):
        panel = panel + move(parts[t], dy=-t).astype(f32)
    panel = panel.astype(bf)
    rows_of = over_y(panel)
    slots = over_z(panel)

    left = after(jnp.concatenate(held[:2], axis=1), panel)
    bands, send_a, send_b = band_products(week, left, wide)

    terms = gram_terms((z - week + n_week) % n_week, rows_of, slots)
    terms = [terms[0]] + [move(terms[j], dw=j) for j in range(1, n_week)]
    got_b = move(after(send_b, *terms[1:]), dw=-1, weeks=(1, 2, 3))
    summed = week_sum(terms, n_y)
    totals = to_rows(summed)
    got_a = move(after(send_a, summed[0]), dw=-1, weeks=(2, 3))

    first = (lax.axis_index("row") * n_col + col) * slim
    last = after(last, *totals)
    bands, here = finish_lag_0(first, last, wide_last, bands, got_b, prior_precision, n_week)

    arrived = [move(here[(1 + j) % n_week], dw=j, weeks=(1,)) for j in range(1, n_week)]
    bands = add_lag_1(bands, got_a)

    ys = [((y + t) % n_y) * 2 + (k + e) % 2 for t in range(n_y) for e in range(2)]
    ys = jnp.stack(ys).astype(jnp.int32)
    schur = place_schur(ys, week, here, arrived, totals)

    return (bands[None], panel, schur)


def solution(mesh):
    placed = (
        P("week", None, None, ("row", "col")),
        P("week", None),
        P("week", None),
        P("week", ("row", "col")),
        P("week", ("row", "col")),
    )
    return jax.shard_map(
        body,
        mesh=mesh,
        in_specs=placed,
        out_specs=(
            P("week", None, ("row", "col"), None),
            P(("row", "col"), "week"),
            P(("row", "col"), "week"),
        ),
        check_vma=False,
    )
```

```python
import jax
import jax.numpy as jnp
from jax import lax
from jax.experimental import pallas as pl
from jax.experimental.pallas import tpu as pltpu
from jax.sharding import PartitionSpec as P

AXES = ("week", "row", "col")


def moved(block, sizes, dw=0, dz=0, dy=0, dk=0, weeks=None):
    n_week, n_row, n_col = sizes
    n_y = n_col // 2
    route = []
    for w in range(n_week):
        if weeks is not None and w not in weeks:
            continue
        for z in range(n_row):
            for y in range(n_y):
                for k in range(2):
                    here = (w * n_row + z) * n_col + y * 2 + k
                    to = (((w + dw) % n_week) * n_row + (z + dz) % n_row) * n_col
                    to += ((y + dy) % n_y) * 2 + (k + dk) % 2
                    route.append((here, to))
    return lax.ppermute(block, AXES, route)


HBM = pl.BlockSpec(memory_space=pl.ANY)
VMEM = pl.BlockSpec(memory_space=pltpu.VMEM)
SMEM = pl.BlockSpec(memory_space=pltpu.SMEM)
LIMIT = pltpu.CompilerParams(vmem_limit_bytes=48 * 1024 * 1024)
bf = jnp.bfloat16
f32 = jnp.float32


def dot_first(left, right):
    return lax.dot_general(
        left, right, (((0,), (0,)), ((), ())), preferred_element_type=jnp.float32
    )


def dot_last(left, right):
    return lax.dot_general(
        left, right, (((1,), (1,)), ((), ())), preferred_element_type=jnp.float32
    )


def brought(copies, sems):
    started = []
    for n, (source, target) in enumerate(copies):
        copy = pltpu.make_async_copy(source, target, sems.at[n])
        copy.start()
        started.append(copy)
    for copy in started:
        copy.wait()


def left_copies(pieces, scratch, a, obs, slim):
    rows = pl.ds(a * obs, obs)
    return [
        (ref, scratch.at[t // 2, rows, pl.ds((t % 2) * slim, slim)])
        for t, ref in enumerate(pieces)
    ]


def right_copies(pieces, scratch, a, obs, slim):
    rows = pl.ds(a * obs, obs)
    return [(ref, scratch.at[rows, pl.ds(n * slim, slim)]) for n, ref in enumerate(pieces)]


def cut(refs, *lengths):
    parts, at = [], 0
    for length in lengths:
        parts.append(refs[at : at + length])
        at += length
    return parts + [refs[at:]]


def coupling_and_parts(lefts, rights, pivots):
    obs, slim = rights[0].shape[1:]
    n_r, n_c, wide = len(lefts), len(rights), pivots[0].shape[0]
    pairs = n_r // 2
    operands, places = list(pivots), []
    for piece in [*lefts, *rights]:
        places.append((len(operands), isinstance(piece, tuple)))
        operands += piece if isinstance(piece, tuple) else [piece]
    n_in = len(operands)

    def kernel(*refs):
        parts, (l_s, r_s, p_s, sems) = refs[n_in : n_in + n_r], refs[n_in + n_r :]
        copies = right_copies(refs[:n_c], p_s, 0, wide, slim)
        for a in range(2):
            blocks = [refs[at + a] if two else refs[at].at[a] for at, two in places]
            copies += left_copies(blocks[:n_r], l_s, a, obs, slim)
            copies += right_copies(blocks[n_r:], r_s, a, obs, slim)
        brought(copies, sems)
        for n in range(pairs):
            block = dot_first(l_s[n], r_s[...]).astype(bf)
            part = dot_last(block, p_s[...])
            for m in range(2):
                out = parts[2 * n + m]
                out[...] = part[m * slim : (m + 1) * slim].astype(out.dtype)

    return pl.pallas_call(
        kernel,
        in_specs=[VMEM] * n_in,
        out_specs=[VMEM] * n_r,
        out_shape=[jax.ShapeDtypeStruct((slim, wide), bf if t else f32) for t in range(n_r)],
        scratch_shapes=[
            pltpu.VMEM((pairs, 2 * obs, 2 * slim), bf),
            pltpu.VMEM((2 * obs, n_c * slim), bf),
            pltpu.VMEM((wide, n_c * slim), bf),
            pltpu.SemaphoreType.DMA((2 * (n_r + n_c) + n_c,)),
        ],
        compiler_params=LIMIT,
        name="coupling_and_parts",
    )(*operands)


def gram_terms(turn, rows_of, slots):
    slim, wide = slots[0].shape
    n_r, n_c = len(rows_of), len(slots)
    pairs, n_j = n_r // 2, n_c // 2

    def kernel(*refs):
        (turn_ref,), l_refs, r_refs, rest = cut(refs, 1, n_r, n_c)
        outs, (l_s, r_s, g_s, sems) = rest[:n_j], rest[n_j:]
        brought(
            [(ref, l_s.at[pl.ds(n * slim, slim)]) for n, ref in enumerate(l_refs)]
            + [(ref, r_s.at[pl.ds(n * slim, slim)]) for n, ref in enumerate(r_refs)],
            sems,
        )
        for n in range(pairs):
            gram = dot_last(l_s[pl.ds(n * 2 * slim, 2 * slim)], r_s[...])
            for e in range(2):
                for s in range(n_j):
                    at = (e * n_j + s) * slim
                    rows, lanes = pl.ds(n * 2 * slim, 2 * slim), pl.ds(e * slim, slim)
                    g_s[s, rows, lanes] = gram[:, at : at + slim]
        for j in range(n_j):
            outs[j][...] = g_s[(turn_ref[0] + n_j - j) % n_j].astype(outs[j].dtype)

    operands = [*rows_of, *slots]
    return pl.pallas_call(
        kernel,
        in_specs=[SMEM] + [VMEM] * len(operands),
        out_specs=[VMEM] * n_j,
        out_shape=[
            jax.ShapeDtypeStruct((n_r * slim, 2 * slim), bf if j else f32) for j in range(n_j)
        ],
        scratch_shapes=[
            pltpu.VMEM((n_r * slim, wide), bf),
            pltpu.VMEM((n_c * slim, wide), bf),
            pltpu.VMEM((n_j, n_r * slim, 2 * slim), f32),
            pltpu.SemaphoreType.DMA((len(operands),)),
        ],
        compiler_params=LIMIT,
        name="gram_terms",
    )(turn.reshape(1), *operands)


def week_sum(terms, n_r):
    rows, wide = terms[0].shape
    slim = rows // n_r

    def kernel(*refs):
        ins, outs = refs[: len(terms)], refs[len(terms) :]
        for n in range(n_r):
            at = pl.ds(n * slim, slim)
            total = ins[0][at].astype(f32)
            for ref in ins[1:]:
                total = total + ref[at].astype(f32)
            outs[n][...] = total.astype(bf)

    return pl.pallas_call(
        kernel,
        in_specs=[VMEM] * len(terms),
        out_specs=[VMEM] * n_r,
        out_shape=[jax.ShapeDtypeStruct((slim, wide), bf)] * n_r,
        name="week_sum",
    )(*terms)


def band_products(week, left, wide):
    n_b, obs, regions = wide.shape
    slim = left.shape[1] // 4
    tile = min(1024, regions // 4)

    def kernel(week_ref, left_ref, wide_ref, band_ref, send_a, send_b, turned):
        @pl.when(pl.program_id(0) == 0)
        def _():
            turned[...] = left_ref[...].T

        from_a = jnp.dot(turned[: 2 * slim], wide_ref[0], preferred_element_type=f32)
        from_b = jnp.dot(turned[2 * slim :], wide_ref[1], preferred_element_type=f32)
        late = week_ref[0] >= 2
        band_ref[0] = jnp.where(late, 0.0, from_a[:slim])
        band_ref[1] = from_b[:slim]
        band_ref[2] = jnp.where(late, from_a[:slim], 0.0)
        send_a[...] = from_a[slim:].astype(bf)
        send_b[...] = from_b[slim:].astype(bf)

    return pl.pallas_call(
        kernel,
        grid=(regions // tile,),
        in_specs=[SMEM, VMEM, pl.BlockSpec((n_b, obs, tile), lambda i: (0, 0, i))],
        out_specs=[
            pl.BlockSpec((3, slim, tile), lambda i: (0, 0, i)),
            pl.BlockSpec((slim, tile), lambda i: (0, i)),
            pl.BlockSpec((slim, tile), lambda i: (0, i)),
        ],
        out_shape=[
            jax.ShapeDtypeStruct((3, slim, regions), f32),
            jax.ShapeDtypeStruct((slim, regions), bf),
            jax.ShapeDtypeStruct((slim, regions), bf),
        ],
        scratch_shapes=[pltpu.VMEM((4 * slim, obs), bf)],
        compiler_params=LIMIT,
        name="band_products",
    )(week.reshape(1), left, wide)


def add_lag_1(bands, arrived):
    _, slim, regions = bands.shape
    tile = min(2048, regions)

    def kernel(band_ref, arrived_ref, out_ref):
        out_ref[0] = band_ref[0] + arrived_ref[...].astype(f32)

    band = pl.BlockSpec((1, slim, tile), lambda i: (1, 0, i))
    return pl.pallas_call(
        kernel,
        grid=(regions // tile,),
        in_specs=[band, pl.BlockSpec((slim, tile), lambda i: (0, i))],
        out_specs=band,
        out_shape=jax.ShapeDtypeStruct(bands.shape, f32),
        input_output_aliases={0: 0},
        name="add_lag_1",
    )(bands, arrived)


def finish_lag_0(first, left, wide, bands, arrived, prior, spans):
    obs, slim = left.shape
    regions = wide.shape[1]
    tile = min(1024, regions // 4)
    span = regions // spans
    each = span // tile

    def kernel(first_ref, left_ref, wide_ref, band_ref, arrived_ref, prior_ref, out_ref, *rest):
        cuts, turned = rest[:spans], rest[spans]
        step = pl.program_id(0)

        @pl.when(step == 0)
        def _():
            turned[...] = left_ref[...].T

        last = jnp.dot(turned[...], wide_ref[...], preferred_element_type=f32)
        rows = lax.broadcasted_iota(jnp.int32, (slim, tile), 0) + first_ref[0]
        cols = lax.broadcasted_iota(jnp.int32, (slim, tile), 1) + step * tile
        total = band_ref[0] + arrived_ref[...].astype(f32) + last
        total = total + jnp.where(rows == cols, prior_ref[...], 0.0)
        out_ref[0] = total
        for n in range(spans):

            @pl.when(step // each == n)
            def _():
                cuts[n][...] = total.astype(bf)

    def cut_spec(n):
        return pl.BlockSpec((slim, tile), lambda i: (0, jnp.clip(i - n * each, 0, each - 1)))

    band = pl.BlockSpec((1, slim, tile), lambda i: (0, 0, i))
    return pl.pallas_call(
        kernel,
        grid=(regions // tile,),
        in_specs=[
            SMEM,
            VMEM,
            pl.BlockSpec((obs, tile), lambda i: (0, i)),
            band,
            pl.BlockSpec((slim, tile), lambda i: (0, i)),
            VMEM,
        ],
        out_specs=[band] + [cut_spec(n) for n in range(spans)],
        out_shape=[jax.ShapeDtypeStruct(bands.shape, f32)]
        + [jax.ShapeDtypeStruct((slim, span), bf)] * spans,
        scratch_shapes=[pltpu.VMEM((slim, obs), bf)],
        input_output_aliases={3: 0},
        compiler_params=LIMIT,
        name="finish_lag_0",
    )(first.reshape(1), left, wide, bands, arrived, prior.reshape(slim, 1))


def place_schur(ys, week, here, arrived, pieces):
    slim = pieces[0].shape[0]
    n, m = len(pieces), len(arrived)

    def kernel(ys_ref, week_ref, here_ref, *refs):
        own = week_ref[0] == 1
        for t in range(n):
            for e in range(2):
                at = pl.ds(pl.multiple_of(ys_ref[2 * t + e] * slim, slim), slim)
                total = -refs[m + t][:, e * slim : (e + 1) * slim].astype(f32)
                total = total + jnp.where(own, here_ref[:, at].astype(f32), 0.0)
                for ref in refs[:m]:
                    total = total + ref[:, at].astype(f32)
                refs[-1][:, at] = total

    return pl.pallas_call(
        kernel,
        in_specs=[SMEM, SMEM] + [VMEM] * (1 + m + n),
        out_specs=VMEM,
        out_shape=jax.ShapeDtypeStruct((slim, 2 * n * slim), f32),
        name="place_schur",
    )(ys, week.reshape(1), here, *arrived, *pieces)


def body(sensitivity, reach, obs_weight, prior_precision, pivot_solve):
    sizes = tuple(lax.axis_size(a) for a in AXES)
    n_week, n_row, n_col = sizes
    n_y = n_col // 2
    week = lax.axis_index("week")
    z = lax.axis_index("row")
    col = lax.axis_index("col")
    y, k = col // 2, col % 2
    local = sensitivity[0]
    lags, obs, slim = local.shape

    def move(block, **by):
        return moved(block, sizes, **by)

    def over_y(block):
        return [block] + [move(block, dy=t) for t in range(1, n_y)]

    def over_z(block):
        own = [block] + [move(block, dz=s) for s in range(1, n_row)]
        return own + [move(p, dk=1) for p in [after(block, own[1])] + own[1:]]

    def to_rows(blocks):
        return [blocks[0]] + [move(blocks[t], dy=-t) for t in range(1, n_y)]

    def after(value, *events):
        return lax.optimization_barrier((value, *events))[0]

    def by_week(*choices):
        return lax.select_n(week, *choices)

    wide = jnp.stack([by_week(local[0], local[0], local[2], local[2]), local[1]])
    wide = lax.all_gather(wide, ("row", "col"), axis=2, tiled=True)
    pivots = over_z(pivot_solve)

    root = jnp.sqrt(obs_weight[0])

    def scaled(lag):
        keep = jnp.where((reach[0] >= lag) & (week >= lag), root, 0.0)
        return (keep[:, None] * local[lag].astype(f32)).astype(bf)

    held = [scaled(lag) for lag in range(lags)]
    pair = jnp.stack(
        [by_week(held[1], held[0], held[1], held[1]), by_week(held[2], held[1], held[2], held[2])]
    )
    below = move(pair, dw=-1, weeks=(1, 2, 3))
    above = move(pair, dw=1, weeks=(1, 2))
    across = move(pair, dw=2, weeks=(1, 2, 3))
    def both(n):
        first = by_week(below[n], pair[n], pair[n], above[n])
        return jnp.stack([first, by_week(across[n], below[n], above[n], across[n])])

    left_c, right_c = over_y(both(0)), over_z(both(1))
    parts = coupling_and_parts(left_c, right_c, pivots)

    last = by_week(across[1], across[1], held[0], held[0])
    last = after(last, parts[0])
    wide_last = lax.all_gather(last, ("row", "col"), axis=1, tiled=True)

    panel = parts[0]
    for t in range(1, n_y):
        panel = panel + move(parts[t], dy=-t).astype(f32)
    panel = panel.astype(bf)
    rows_of = over_y(panel)
    slots = over_z(panel)

    weight = [
        jnp.where((reach[0] >= lag) & (week >= lag), obs_weight[0], 0.0) for lag in range(lags)
    ]
    weight = (by_week(weight[0], weight[0], weight[2], weight[2]), weight[1])
    left = [
        (weight[b][:, None] * local[a].astype(f32)).astype(bf) for b in range(2) for a in range(2)
    ]
    left = after(jnp.concatenate(left, axis=1), panel)
    bands, send_a, send_b = band_products(week, left, wide)

    terms = gram_terms((z - week + n_week) % n_week, rows_of, slots)
    terms = [terms[0]] + [move(terms[j], dw=j) for j in range(1, n_week)]
    got_b = move(after(send_b, *terms[1:]), dw=-1, weeks=(1, 2, 3))
    summed = week_sum(terms, n_y)
    totals = to_rows(summed)
    got_a = move(after(send_a, summed[0]), dw=-1, weeks=(2, 3))

    first = (lax.axis_index("row") * n_col + col) * slim
    last = after(last, *totals)
    bands, *here = finish_lag_0(first, last, wide_last, bands, got_b, prior_precision, n_week)

    arrived = [move(here[(1 + j) % n_week], dw=j, weeks=(1,)) for j in range(1, n_week)]
    bands = add_lag_1(bands, got_a)

    ys = [((y + t) % n_y) * 2 + (k + e) % 2 for t in range(n_y) for e in range(2)]
    ys = jnp.stack(ys).astype(jnp.int32)
    schur = place_schur(ys, week, here[1], arrived, totals)

    return (bands[None], panel, schur)


def solution(mesh):
    placed = (
        P("week", None, None, ("row", "col")),
        P("week", None),
        P("week", None),
        P("week", ("row", "col")),
        P("week", ("row", "col")),
    )
    return jax.shard_map(
        body,
        mesh=mesh,
        in_specs=placed,
        out_specs=(
            P("week", None, ("row", "col"), None),
            P(("row", "col"), "week"),
            P(("row", "col"), "week"),
        ),
        check_vma=False,
    )
```

```python
import jax
import jax.numpy as jnp
from jax import lax
from jax.experimental import pallas as pl
from jax.experimental.pallas import tpu as pltpu
from jax.sharding import PartitionSpec as P

AXES = ("week", "row", "col")


def moved(block, sizes, dw=0, dz=0, dy=0, dk=0, weeks=None):
    n_week, n_row, n_col = sizes
    n_y = n_col // 2
    route = []
    for w in range(n_week):
        if weeks is not None and w not in weeks:
            continue
        for z in range(n_row):
            for y in range(n_y):
                for k in range(2):
                    here = (w * n_row + z) * n_col + y * 2 + k
                    to = (((w + dw) % n_week) * n_row + (z + dz) % n_row) * n_col
                    to += ((y + dy) % n_y) * 2 + (k + dk) % 2
                    route.append((here, to))
    return lax.ppermute(block, AXES, route)


HBM = pl.BlockSpec(memory_space=pl.ANY)
VMEM = pl.BlockSpec(memory_space=pltpu.VMEM)
SMEM = pl.BlockSpec(memory_space=pltpu.SMEM)
LIMIT = pltpu.CompilerParams(vmem_limit_bytes=48 * 1024 * 1024)
bf = jnp.bfloat16
f32 = jnp.float32


def dot_first(left, right):
    return lax.dot_general(
        left, right, (((0,), (0,)), ((), ())), preferred_element_type=jnp.float32
    )


def dot_last(left, right):
    return lax.dot_general(
        left, right, (((1,), (1,)), ((), ())), preferred_element_type=jnp.float32
    )


def brought(copies, sems):
    started = []
    for n, (source, target) in enumerate(copies):
        copy = pltpu.make_async_copy(source, target, sems.at[n])
        copy.start()
        started.append(copy)
    for copy in started:
        copy.wait()


def left_copies(pieces, scratch, a, obs, slim):
    rows = pl.ds(a * obs, obs)
    return [
        (ref, scratch.at[t // 2, rows, pl.ds((t % 2) * slim, slim)])
        for t, ref in enumerate(pieces)
    ]


def right_copies(pieces, scratch, a, obs, slim):
    rows = pl.ds(a * obs, obs)
    return [(ref, scratch.at[rows, pl.ds(n * slim, slim)]) for n, ref in enumerate(pieces)]


def cut(refs, *lengths):
    parts, at = [], 0
    for length in lengths:
        parts.append(refs[at : at + length])
        at += length
    return parts + [refs[at:]]


def coupling_and_parts(lefts, rights, pivots):
    obs, slim = rights[0].shape[1:]
    n_r, n_c, wide = len(lefts), len(rights), pivots[0].shape[0]
    pairs = n_r // 2
    operands, places = list(pivots), []
    for piece in [*lefts, *rights]:
        places.append((len(operands), isinstance(piece, tuple)))
        operands += piece if isinstance(piece, tuple) else [piece]
    n_in = len(operands)

    def kernel(*refs):
        parts, (l_s, r_s, p_s, sems) = refs[n_in : n_in + n_r], refs[n_in + n_r :]
        copies = right_copies(refs[:n_c], p_s, 0, wide, slim)
        for a in range(2):
            blocks = [refs[at + a] if two else refs[at].at[a] for at, two in places]
            copies += left_copies(blocks[:n_r], l_s, a, obs, slim)
            copies += right_copies(blocks[n_r:], r_s, a, obs, slim)
        brought(copies, sems)
        for n in range(pairs):
            block = dot_first(l_s[n], r_s[...]).astype(bf)
            part = dot_last(block, p_s[...])
            for m in range(2):
                out = parts[2 * n + m]
                out[...] = part[m * slim : (m + 1) * slim].astype(out.dtype)

    return pl.pallas_call(
        kernel,
        in_specs=[VMEM] * n_in,
        out_specs=[VMEM] * n_r,
        out_shape=[jax.ShapeDtypeStruct((slim, wide), bf if t else f32) for t in range(n_r)],
        scratch_shapes=[
            pltpu.VMEM((pairs, 2 * obs, 2 * slim), bf),
            pltpu.VMEM((2 * obs, n_c * slim), bf),
            pltpu.VMEM((wide, n_c * slim), bf),
            pltpu.SemaphoreType.DMA((2 * (n_r + n_c) + n_c,)),
        ],
        compiler_params=LIMIT,
        name="coupling_and_parts",
    )(*operands)


def gram_terms(turn, rows_of, slots):
    slim, wide = slots[0].shape
    n_r, n_c = len(rows_of), len(slots)
    pairs, n_j = n_r // 2, n_c // 2

    def kernel(*refs):
        (turn_ref,), l_refs, r_refs, rest = cut(refs, 1, n_r, n_c)
        outs, (l_s, r_s, g_s, sems) = rest[:n_j], rest[n_j:]
        brought(
            [(ref, l_s.at[pl.ds(n * slim, slim)]) for n, ref in enumerate(l_refs)]
            + [(ref, r_s.at[pl.ds(n * slim, slim)]) for n, ref in enumerate(r_refs)],
            sems,
        )
        for n in range(pairs):
            gram = dot_last(l_s[pl.ds(n * 2 * slim, 2 * slim)], r_s[...])
            for e in range(2):
                for s in range(n_j):
                    at = (e * n_j + s) * slim
                    rows, lanes = pl.ds(n * 2 * slim, 2 * slim), pl.ds(e * slim, slim)
                    g_s[s, rows, lanes] = gram[:, at : at + slim]
        for j in range(n_j):
            outs[j][...] = g_s[(turn_ref[0] + n_j - j) % n_j].astype(outs[j].dtype)

    operands = [*rows_of, *slots]
    return pl.pallas_call(
        kernel,
        in_specs=[SMEM] + [VMEM] * len(operands),
        out_specs=[VMEM] * n_j,
        out_shape=[
            jax.ShapeDtypeStruct((n_r * slim, 2 * slim), bf if j else f32) for j in range(n_j)
        ],
        scratch_shapes=[
            pltpu.VMEM((n_r * slim, wide), bf),
            pltpu.VMEM((n_c * slim, wide), bf),
            pltpu.VMEM((n_j, n_r * slim, 2 * slim), f32),
            pltpu.SemaphoreType.DMA((len(operands),)),
        ],
        compiler_params=LIMIT,
        name="gram_terms",
    )(turn.reshape(1), *operands)


def week_sum(terms, n_r):
    rows, wide = terms[0].shape
    slim = rows // n_r

    def kernel(*refs):
        ins, outs = refs[: len(terms)], refs[len(terms) :]
        for n in range(n_r):
            at = pl.ds(n * slim, slim)
            total = ins[0][at].astype(f32)
            for ref in ins[1:]:
                total = total + ref[at].astype(f32)
            outs[n][...] = total.astype(bf)

    return pl.pallas_call(
        kernel,
        in_specs=[VMEM] * len(terms),
        out_specs=[VMEM] * n_r,
        out_shape=[jax.ShapeDtypeStruct((slim, wide), bf)] * n_r,
        name="week_sum",
    )(*terms)


def band_products(week, left, wide):
    n_b, obs, regions = wide.shape
    slim = left.shape[1] // 4
    tile = min(1024, regions // 4)

    def kernel(week_ref, left_ref, wide_ref, band_ref, send_a, send_b, turned):
        @pl.when(pl.program_id(0) == 0)
        def _():
            turned[...] = left_ref[...].T

        from_a = jnp.dot(turned[: 2 * slim], wide_ref[0], preferred_element_type=f32)
        from_b = jnp.dot(turned[2 * slim :], wide_ref[1], preferred_element_type=f32)
        late = week_ref[0] >= 2
        band_ref[0] = jnp.where(late, 0.0, from_a[:slim])
        band_ref[1] = from_b[:slim]
        band_ref[2] = jnp.where(late, from_a[:slim], 0.0)
        send_a[...] = from_a[slim:].astype(bf)
        send_b[...] = from_b[slim:].astype(bf)

    return pl.pallas_call(
        kernel,
        grid=(regions // tile,),
        in_specs=[SMEM, VMEM, pl.BlockSpec((n_b, obs, tile), lambda i: (0, 0, i))],
        out_specs=[
            pl.BlockSpec((3, slim, tile), lambda i: (0, 0, i)),
            pl.BlockSpec((slim, tile), lambda i: (0, i)),
            pl.BlockSpec((slim, tile), lambda i: (0, i)),
        ],
        out_shape=[
            jax.ShapeDtypeStruct((3, slim, regions), f32),
            jax.ShapeDtypeStruct((slim, regions), bf),
            jax.ShapeDtypeStruct((slim, regions), bf),
        ],
        scratch_shapes=[pltpu.VMEM((4 * slim, obs), bf)],
        compiler_params=LIMIT,
        name="band_products",
    )(week.reshape(1), left, wide)


def add_lag_1(bands, arrived):
    _, slim, regions = bands.shape
    tile = min(2048, regions)

    def kernel(band_ref, arrived_ref, out_ref):
        out_ref[0] = band_ref[0] + arrived_ref[...].astype(f32)

    band = pl.BlockSpec((1, slim, tile), lambda i: (1, 0, i))
    return pl.pallas_call(
        kernel,
        grid=(regions // tile,),
        in_specs=[band, pl.BlockSpec((slim, tile), lambda i: (0, i))],
        out_specs=band,
        out_shape=jax.ShapeDtypeStruct(bands.shape, f32),
        input_output_aliases={0: 0},
        name="add_lag_1",
    )(bands, arrived)


def finish_lag_0(first, left, wide, bands, arrived, prior, spans):
    obs, slim = left.shape
    regions = wide.shape[1]
    tile = min(1024, regions // 4)
    span = regions // spans
    each = span // tile

    def kernel(first_ref, left_ref, wide_ref, band_ref, arrived_ref, prior_ref, out_ref, *rest):
        cuts, turned = rest[:spans], rest[spans]
        step = pl.program_id(0)

        @pl.when(step == 0)
        def _():
            turned[...] = left_ref[...].T

        last = jnp.dot(turned[...], wide_ref[...], preferred_element_type=f32)
        rows = lax.broadcasted_iota(jnp.int32, (slim, tile), 0) + first_ref[0]
        cols = lax.broadcasted_iota(jnp.int32, (slim, tile), 1) + step * tile
        total = band_ref[0] + arrived_ref[...].astype(f32) + last
        total = total + jnp.where(rows == cols, prior_ref[...], 0.0)
        out_ref[0] = total
        for n in range(spans):

            @pl.when(step // each == n)
            def _():
                cuts[n][...] = total.astype(bf)

    def cut_spec(n):
        return pl.BlockSpec((slim, tile), lambda i: (0, jnp.clip(i - n * each, 0, each - 1)))

    band = pl.BlockSpec((1, slim, tile), lambda i: (0, 0, i))
    return pl.pallas_call(
        kernel,
        grid=(regions // tile,),
        in_specs=[
            SMEM,
            VMEM,
            pl.BlockSpec((obs, tile), lambda i: (0, i)),
            band,
            pl.BlockSpec((slim, tile), lambda i: (0, i)),
            VMEM,
        ],
        out_specs=[band] + [cut_spec(n) for n in range(spans)],
        out_shape=[jax.ShapeDtypeStruct(bands.shape, f32)]
        + [jax.ShapeDtypeStruct((slim, span), bf)] * spans,
        scratch_shapes=[pltpu.VMEM((slim, obs), bf)],
        input_output_aliases={3: 0},
        compiler_params=LIMIT,
        name="finish_lag_0",
    )(first.reshape(1), left, wide, bands, arrived, prior.reshape(slim, 1))


def place_schur(ys, week, here, arrived, pieces):
    slim = pieces[0].shape[0]
    n, m = len(pieces), len(arrived)

    def kernel(ys_ref, week_ref, here_ref, *refs):
        own = week_ref[0] == 1
        for t in range(n):
            for e in range(2):
                at = pl.ds(pl.multiple_of(ys_ref[2 * t + e] * slim, slim), slim)
                total = -refs[m + t][:, e * slim : (e + 1) * slim].astype(f32)
                total = total + jnp.where(own, here_ref[:, at].astype(f32), 0.0)
                for ref in refs[:m]:
                    total = total + ref[:, at].astype(f32)
                refs[-1][:, at] = total

    return pl.pallas_call(
        kernel,
        in_specs=[SMEM, SMEM] + [VMEM] * (1 + m + n),
        out_specs=VMEM,
        out_shape=jax.ShapeDtypeStruct((slim, 2 * n * slim), f32),
        name="place_schur",
    )(ys, week.reshape(1), here, *arrived, *pieces)


def body(sensitivity, reach, obs_weight, prior_precision, pivot_solve):
    sizes = tuple(lax.axis_size(a) for a in AXES)
    n_week, n_row, n_col = sizes
    n_y = n_col // 2
    week = lax.axis_index("week")
    z = lax.axis_index("row")
    col = lax.axis_index("col")
    y, k = col // 2, col % 2
    local = sensitivity[0]
    lags, obs, slim = local.shape

    def move(block, **by):
        return moved(block, sizes, **by)

    def over_y(block):
        return [block] + [move(block, dy=t) for t in range(1, n_y)]

    def over_z(block):
        own = [block] + [move(block, dz=s) for s in range(1, n_row)]
        return own + [move(p, dk=1) for p in [after(block, own[1])] + own[1:]]

    def to_rows(blocks):
        return [blocks[0]] + [move(blocks[t], dy=-t) for t in range(1, n_y)]

    def after(value, *events):
        return lax.optimization_barrier((value, *events))[0]

    def by_week(*choices):
        return lax.select_n(week, *choices)

    wide = jnp.stack([by_week(local[0], local[0], local[2], local[2]), local[1]])
    wide = lax.all_gather(wide, ("row", "col"), axis=2, tiled=True)
    pivots = over_z(pivot_solve)

    root = jnp.sqrt(obs_weight[0])

    def scaled(lag):
        keep = jnp.where((reach[0] >= lag) & (week >= lag), root, 0.0)
        return (keep[:, None] * local[lag].astype(f32)).astype(bf)

    held = [scaled(lag) for lag in range(lags)]
    pair = jnp.stack(
        [by_week(held[1], held[0], held[1], held[1]), by_week(held[2], held[1], held[2], held[2])]
    )
    below = move(pair, dw=-1, weeks=(1, 2, 3))
    above = move(pair, dw=1, weeks=(1, 2))
    across = move(pair, dw=2, weeks=(1, 2, 3))
    def both(n):
        first = by_week(below[n], pair[n], pair[n], above[n])
        return jnp.stack([first, by_week(across[n], below[n], above[n], across[n])])

    left_c, right_c = over_y(both(0)), over_z(both(1))
    parts = coupling_and_parts(left_c, right_c, pivots)

    last = by_week(across[1], across[1], held[0], held[0])
    last = after(last, parts[0])
    wide_last = lax.all_gather(last, ("row", "col"), axis=1, tiled=True)

    panel = parts[0]
    for t in range(1, n_y):
        panel = panel + move(parts[t], dy=-t).astype(f32)
    panel = panel.astype(bf)
    rows_of = over_y(panel)
    slots = over_z(panel)

    weight = [
        jnp.where((reach[0] >= lag) & (week >= lag), obs_weight[0], 0.0) for lag in range(lags)
    ]
    weight = (by_week(weight[0], weight[0], weight[2], weight[2]), weight[1])
    left = [
        (weight[b][:, None] * local[a].astype(f32)).astype(bf) for b in range(2) for a in range(2)
    ]
    left = after(jnp.concatenate(left, axis=1), panel)
    bands, send_a, send_b = band_products(week, left, wide)

    terms = gram_terms((z - week + n_week) % n_week, rows_of, slots)
    terms = [terms[0]] + [move(terms[j], dw=j) for j in range(1, n_week)]
    got_b = move(after(send_b, *terms[1:]), dw=-1, weeks=(1, 2, 3))
    summed = week_sum(terms, n_y)
    totals = to_rows(summed)
    got_a = move(after(send_a, summed[0]), dw=-1, weeks=(2, 3))

    first = (lax.axis_index("row") * n_col + col) * slim
    last = after(last, *totals)
    bands, *here = finish_lag_0(first, last, wide_last, bands, got_b, prior_precision, n_week)

    arrived = [move(here[(1 + j) % n_week], dw=j, weeks=(1,)) for j in range(1, n_week)]

    ys = [((y + t) % n_y) * 2 + (k + e) % 2 for t in range(n_y) for e in range(2)]
    ys = jnp.stack(ys).astype(jnp.int32)
    schur = place_schur(ys, week, here[1], arrived, totals)

    bands = add_lag_1(after(bands, schur), got_a)
    return (bands[None], panel, schur)


def solution(mesh):
    placed = (
        P("week", None, None, ("row", "col")),
        P("week", None),
        P("week", None),
        P("week", ("row", "col")),
        P("week", ("row", "col")),
    )
    return jax.shard_map(
        body,
        mesh=mesh,
        in_specs=placed,
        out_specs=(
            P("week", None, ("row", "col"), None),
            P(("row", "col"), "week"),
            P(("row", "col"), "week"),
        ),
        check_vma=False,
    )
```
